32 devices in a mesh: groups: 2 (over y), seq: 8 (over z, x), tensor: 2 (over core).
Axes of the slice: x: 2, y: 2, z: 4, core: 2. Of those that a mesh axis runs over, the one named last changes fastest.
Arguments:
- strain: float32 [3, 14336], P(None, ('groups', 'seq')), parts along dimension 1, may hold values from -6 to 6
- offsets: int32 [6], P('groups'), parts along dimension 0, may hold values from 0 to 128, as said below
- dilation: int32 [2], replicated, may hold values from 1 to 512, as said below
- input_weight: float32 [3, 512], replicated, may hold values from -3.5 to 3.5
- conv_weight: bfloat16 [2, 1024, 2, 512], P(None, None, None, 'tensor'), may hold values from -0.1875 to 0.1875
- conv_bias: float32 [2, 2, 512], P(None, None, 'tensor'), may hold values from -3 to 3
- out_weight: bfloat16 [2, 512, 512], P(None, 'tensor'), may hold values from -0.25 to 0.25
- cotangent: bfloat16 [14336, 512], P(('groups', 'seq')), parts along dimension 0, may hold values from -6 to 6
Outputs:
- grad_input: float32 [6, 512], P('groups'), parts along dimension 0
- grad_conv: float32 [4, 1024, 2, 512], P('groups', 'seq', None, 'tensor'), parts along dimension 0
- grad_bias: float32 [4, 2, 512], P('groups', None, 'tensor'), parts along dimension 0
- grad_out: float32 [4, 512, 512], P('groups', 'tensor'), parts along dimension 0
The draws below stay inside these ranges and needn't reach their ends.
There are 2 independent parts, one for each index of `groups`. The reference program is written for one: setup_inputs(seed, part) draws one part's arguments, and reference() takes and returns one part's arrays. A program takes and returns all parts, laid end to end along the dimension named above; an argument that names none is the same for every part. Nothing has to cross between parts.
Inputs may be any that keep to these rules, and one draw needn't show every extreme that they name: `offsets`: one detector's delay is exactly 128. Powers of two; exactly one layer's dilation is 2 ** 9.
All inputs are finite; a program needn't handle non-finite values.
Results may differ from the reference program's by a relative error of at most 0.01.
Values may be sent and summed in bfloat16 or wider, within the bound.
No kernel may reach another device: no remote copies, remote signals or barrier semaphores. Data moves between devices by JAX's collectives and lax.ppermute only.
A program may use at most 64 MiB of HBM per device.

```python
import math
import jax
import jax.numpy as jnp
from jax import lax

CH = 512
DET = 3
RESIDUAL_LAYERS = 2
DILATION_EXPONENT = 9
MAXSHIFT = 128
SAMPLES = 7168
N_TENSOR = 2


def draw_offsets(key, part):
    random_key_list, key_choice = jax.random.split(jax.random.fold_in(key, 11))
    values = jax.random.randint(random_key_list, (DET,), 0, MAXSHIFT + 1)
    picked_lags = jax.random.randint(key_choice, (), 0, DET)
    return jnp.where(jnp.arange(DET) == picked_lags, MAXSHIFT, values).astype(jnp.int32)


def draw_dilation(key, part):
    random_key_list, key_choice = jax.random.split(jax.random.fold_in(key, 23))
    dilation_factors = jax.random.randint(random_key_list, (RESIDUAL_LAYERS,), 0, DILATION_EXPONENT)
    picked_lags = jax.random.randint(key_choice, (), 0, RESIDUAL_LAYERS)
    dilation_factors = jnp.where(jnp.arange(RESIDUAL_LAYERS) == picked_lags, DILATION_EXPONENT, dilation_factors).astype(jnp.int32)
    return jnp.left_shift(jnp.ones((RESIDUAL_LAYERS,), jnp.int32), dilation_factors)


def level_of(stream_key, extent, cuts, least, high):
    def one(position, blocks):
        draws = jax.random.uniform(jax.random.fold_in(jax.random.fold_in(stream_key, 6), position), (blocks,), jnp.float32, least / len(cuts), high / len(cuts))
        return jnp.repeat(jnp.exp(draws), extent[position] // blocks).reshape((-1,) + (1,) * (len(extent) - position - 1))

    factor_of = one(*cuts[0])
    for cut in cuts[1:]:
        factor_of = factor_of * one(*cut)
    return factor_of


def scatter_about(key, extent, deviation, limit, pieces=(), held_as=jnp.bfloat16):
    result = deviation * jax.random.normal(key, extent, jnp.float32)
    if pieces:
        result = result * level_of(key, extent, pieces, -0.22, 0.18)
    return jnp.clip(result, -limit, limit).astype(held_as)


def setup_inputs(seed: int = 0, part: int = 0) -> dict:
    key_list = jax.random.split(jax.random.key(seed), 9)
    part_keys = jax.random.split(jax.random.fold_in(key_list[8], part), 9)
    strain = scatter_about(part_keys[0], (DET, SAMPLES), 1.0, 6.0, ((1, 8),), jnp.float32)
    offsets = draw_offsets(jax.random.fold_in(jax.random.fold_in(key_list[8], part), 71), part)
    dilation = draw_dilation(jax.random.fold_in(key_list[8], 71), part)
    input_weight = scatter_about(key_list[3], (DET, CH), DET ** -0.5, 3.5, (), jnp.float32)
    conv_weight = scatter_about(key_list[4], (RESIDUAL_LAYERS, 2 * CH, 2, CH), (2 * CH) ** -0.5, 0.1875, ((3, 2),))
    conv_bias = scatter_about(key_list[5], (RESIDUAL_LAYERS, 2, CH), 0.5, 3.0, ((2, 2),), jnp.float32)
    out_weight = scatter_about(key_list[6], (RESIDUAL_LAYERS, CH, CH), CH ** -0.5, 0.25, ((1, 2),))
    cotangent = scatter_about(part_keys[7], (SAMPLES, CH), 1.0, 6.0, ((0, 8),))
    return dict(strain=strain, offsets=offsets, dilation=dilation, input_weight=input_weight, conv_weight=conv_weight, conv_bias=conv_bias, out_weight=out_weight, cotangent=cotangent)


def delayed(values, amount):
    row_count = values.shape[0]
    border_filled = jnp.concatenate([jnp.zeros_like(values), values], axis=0)
    return lax.dynamic_slice_in_dim(border_filled, (row_count - amount).astype(jnp.int32), row_count, 0)

def advanced(values, amount):
    row_count = values.shape[0]
    border_filled = jnp.concatenate([values, jnp.zeros_like(values)], axis=0)
    return lax.dynamic_slice_in_dim(border_filled, amount.astype(jnp.int32), row_count, 0)

def block_sum(block_terms):
    rounded = lax.optimization_barrier(block_terms.astype(jnp.bfloat16))
    return lax.optimization_barrier(jnp.sum(rounded.astype(jnp.float32), axis=1))

def reference(strain, offsets, dilation, input_weight, conv_weight, conv_bias, out_weight, cotangent):
    blocks = N_TENSOR
    block_width = CH // blocks
    signal = jnp.stack([delayed(strain[detector], offsets[detector]) for detector in range(DET)])
    hidden = lax.dot_general(signal, input_weight, (((0,), (0,)), ((), ())), precision=lax.Precision.HIGHEST, preferred_element_type=jnp.float32).astype(jnp.bfloat16)
    stored = []
    for layer_idx in range(RESIDUAL_LAYERS):
        lagged = delayed(hidden, dilation[layer_idx])
        joined = jnp.concatenate([lagged, hidden], axis=1)
        preact = jnp.dot(joined, conv_weight[layer_idx].reshape(2 * CH, 2 * CH), preferred_element_type=jnp.float32).reshape(SAMPLES, 2, CH) + conv_bias[layer_idx]
        gate_out = (jnp.tanh(preact[:, 0]) * jax.nn.sigmoid(preact[:, 1])).astype(jnp.bfloat16)
        parts_mix = jnp.einsum('sjw,jwc->sjc', gate_out.reshape(SAMPLES, blocks, block_width).astype(jnp.float32), out_weight[layer_idx].reshape(blocks, block_width, CH).astype(jnp.float32))
        hidden = (hidden.astype(jnp.float32) + block_sum(parts_mix)).astype(jnp.bfloat16)
        stored.append((joined, preact, gate_out))
    adjoint = cotangent.astype(jnp.float32) * (1.0 / math.sqrt(SAMPLES))
    conv_grads = []
    bias_grads = []
    out_grads = []
    for layer_idx in reversed(range(RESIDUAL_LAYERS)):
        joined, preact, gate_out = stored[layer_idx]
        adjoint_low = adjoint.astype(jnp.bfloat16)
        grad_gated = lax.dot_general(adjoint_low, out_weight[layer_idx], (((1,), (1,)), ((), ())), preferred_element_type=jnp.float32)
        out_grads.insert(0, lax.dot_general(gate_out, adjoint_low, (((0,), (0,)), ((), ())), preferred_element_type=jnp.float32))
        tanh_part = jnp.tanh(preact[:, 0])
        sigm_part = jax.nn.sigmoid(preact[:, 1])
        grad_pre = jnp.stack([grad_gated * sigm_part * (1.0 - tanh_part * tanh_part), grad_gated * tanh_part * sigm_part * (1.0 - sigm_part)], axis=1)
        bias_grads.insert(0, lax.optimization_barrier(jnp.sum(grad_pre, axis=0)))
        grad_low = grad_pre.astype(jnp.bfloat16)
        leading = advanced(grad_low, dilation[layer_idx])
        weight_now = conv_weight[layer_idx].astype(jnp.float32).reshape(2 * CH, 2, blocks, block_width)
        block_terms = jnp.einsum('sgjw,cgjw->sjc', grad_low.reshape(SAMPLES, 2, blocks, block_width).astype(jnp.float32), weight_now[CH:])
        block_terms = block_terms + jnp.einsum('sgjw,cgjw->sjc', leading.reshape(SAMPLES, 2, blocks, block_width).astype(jnp.float32), weight_now[:CH])
        adjoint = adjoint + block_sum(block_terms)
        conv_grads.insert(0, lax.dot_general(joined, grad_low.reshape(SAMPLES, 2 * CH), (((0,), (0,)), ((), ())), preferred_element_type=jnp.float32).reshape(2 * CH, 2, CH))
    grad_input = lax.dot_general(signal, adjoint, (((1,), (0,)), ((), ())), precision=lax.Precision.HIGHEST, preferred_element_type=jnp.float32)
    return (grad_input, jnp.stack(conv_grads), jnp.stack(bias_grads), jnp.stack(out_grads))
```

```python
import math

import jax
import jax.numpy as jnp
from jax import lax
from jax.sharding import PartitionSpec as P

DET = 3
DILATION_EXPONENT = 9
MAXSHIFT = 128
LAG = 2**DILATION_EXPONENT
F32 = jnp.float32
BF16 = jnp.bfloat16


def dot(a, b, dims):
    return lax.dot_general(a, b, (dims, ((), ())), preferred_element_type=F32)


def top(x):
    return lax.reduce_precision(x, 8, 7)


def parts(x):
    hi = top(x)
    return hi.astype(BF16), top(x - hi).astype(BF16)


def swap(x):
    return lax.ppermute(x, "tensor", [(0, 1), (1, 0)])


def gates(pre, width):
    return jnp.tanh(pre[:, :width]), jax.nn.sigmoid(pre[:, width:])


def slopes(gg, th, sg):
    return jnp.concatenate([gg * sg * (1.0 - th * th), gg * th * sg * (1.0 - sg)], axis=1)


def scatter_sum(x, n):
    blocks = x.astype(BF16).reshape(n, x.shape[0] // n, x.shape[1])
    got = lax.all_to_all(blocks, "seq", 0, 0, tiled=True)
    return jnp.sum(got.astype(F32), axis=0)


def gather(x, n):
    got = lax.all_to_all(jnp.broadcast_to(x[None], (n,) + x.shape), "seq", 0, 0, tiled=True)
    return got


def body(strain, offsets, dilation, input_weight, conv_weight, conv_bias, out_weight, cotangent):
    rows = strain.shape[1]
    channels = input_weight.shape[1]
    width = conv_weight.shape[3]
    n = lax.axis_size("seq")
    me = lax.axis_index("seq")
    ext = LAG + rows
    scale = 1.0 / math.sqrt(rows * n)
    inside = jnp.where(me == 0, 0.0, 1.0)
    keep = jnp.where(lax.broadcasted_iota(jnp.int32, (ext, 1), 0) < LAG, inside, 1.0)

    prev = lax.ppermute(strain, "seq", [(i, i + 1) for i in range(n - 1)])
    spare = 2 * LAG + MAXSHIFT - rows
    line = jnp.concatenate([jnp.zeros((DET, spare), F32), prev, strain], axis=1)
    starts = [LAG + MAXSHIFT - offsets[k] for k in range(DET)]
    sig = jnp.stack(
        [lax.dynamic_slice_in_dim(line[k], starts[k] - dilation[0], ext, 0) for k in range(DET)]
        + [lax.dynamic_slice_in_dim(line[k], starts[k], ext, 0) for k in range(DET)]
    )
    s_hi, s_lo = parts(sig)
    s3 = jnp.concatenate([s_hi, s_lo, s_hi], axis=0)

    w0 = conv_weight[0].reshape(2 * channels, 2 * width)
    w1 = conv_weight[1].reshape(2 * channels, 2 * width)
    b0 = conv_bias[0].reshape(2 * width)
    b1 = conv_bias[1].reshape(2 * width)
    i_hi, i_lo = parts(input_weight)
    i2 = jnp.concatenate([i_hi, i_lo], axis=0)
    a_lag = dot(i2, w0[:channels], ((1,), (0,)))
    a_cur = dot(i2, w0[channels:], ((1,), (0,)))
    a0 = jnp.concatenate([a_lag[:DET] + a_lag[DET:], a_cur[:DET] + a_cur[DET:]], axis=0)
    a_hi, a_lo = parts(a0)
    a3 = jnp.concatenate([a_hi, a_hi, a_lo], axis=0)

    pre0 = dot(s3, a3, ((0,), (0,))) + b0
    th0, sg0 = gates(pre0, width)
    gate0 = (th0 * sg0).astype(BF16)
    mine = dot(gate0, out_weight[0], ((1,), (0,))).astype(BF16)
    other = swap(mine)
    c3 = jnp.concatenate([s_hi[DET:], s_lo[DET:], s_hi[DET:]], axis=0)
    h0 = dot(c3, jnp.concatenate([i_hi, i_hi, i_lo], axis=0), ((0,), (0,)))
    h1 = ((h0 + mine.astype(F32) + other.astype(F32)) * keep).astype(BF16)

    lag1 = lax.dynamic_slice_in_dim(h1, LAG - dilation[1], rows, 0)
    cur1 = h1[LAG:]
    pre1 = dot(lag1, w1[:channels], ((1,), (0,))) + dot(cur1, w1[channels:], ((1,), (0,))) + b1
    th1, sg1 = gates(pre1, width)
    gate1 = (th1 * sg1).astype(BF16)
    gg1 = dot(cotangent, out_weight[1], ((1,), (1,))) * scale
    gp1 = slopes(gg1, th1, sg1)
    gl1 = gp1.astype(BF16)
    c_cur = dot(gl1, w1[channels:], ((1,), (1,)))
    c_lag = dot(gl1, w1[:channels], ((1,), (1,)))
    base = jnp.concatenate([jnp.zeros((LAG, channels), F32), c_cur], axis=0)
    moved = lax.dynamic_slice_in_dim(
        jnp.concatenate(
            [jnp.zeros((LAG, channels), F32), c_lag, jnp.zeros((LAG, channels), F32)], axis=0
        ),
        dilation[1],
        ext,
        0,
    )
    part = (base + moved).astype(BF16)
    apart = swap(part)

    dw_lag = dot(lag1, gl1, ((0,), (0,)))
    dw_cur = dot(cur1, gl1, ((0,), (0,)))
    dw1 = scatter_sum(jnp.concatenate([dw_lag, dw_cur], axis=0), n)
    do1 = scatter_sum(dot(gate1, cotangent, ((0,), (0,))) * scale, n)

    cot_ext = jnp.concatenate([jnp.zeros((LAG, channels), BF16), cotangent], axis=0)
    adj = part.astype(F32) + apart.astype(F32) + cot_ext.astype(F32) * scale
    adj = (adj * keep).astype(BF16)
    gg0 = dot(adj, out_weight[0], ((1,), (1,)))
    gp0 = slopes(gg0, th0, sg0)
    gl0 = gp0.astype(BF16)
    do0 = scatter_sum(dot(gate0, adj, ((0,), (0,))), n)
    s2 = jnp.concatenate([s_hi, s_lo], axis=0)
    r2 = dot(s2, gl0, ((1,), (0,)))
    r = r2[: 2 * DET] + r2[2 * DET :]
    g2 = dot(jnp.concatenate([s_hi[DET:], s_lo[DET:]], axis=0), adj, ((1,), (0,)))
    first = jnp.where(lax.axis_index("tensor") == 0, 1.0, 0.0)
    g = (g2[:DET] + g2[DET:]) * first
    r_hi, r_lo = parts(r)
    back = dot(jnp.concatenate([r_hi[:DET], r_lo[:DET]], axis=0), w0[:channels], ((1,), (1,)))
    back += dot(jnp.concatenate([r_hi[DET:], r_lo[DET:]], axis=0), w0[channels:], ((1,), (1,)))
    g = g + back[:DET] + back[DET:]
    bias = jnp.stack([jnp.sum(gp0, axis=0), jnp.sum(gp1, axis=0)])
    small = gather(jnp.concatenate([r, g, bias], axis=0), n)
    small = jnp.sum(small, axis=0)
    r, g, bias = small[: 2 * DET], small[2 * DET : 3 * DET], small[3 * DET :]
    grad_input = g + swap(g)
    grad_bias = bias.reshape(2, 2, width)
    block = 2 * channels // n
    mine_iw = lax.dynamic_slice_in_dim(input_weight, (me * block) % channels, block, 1)
    mine_r = jnp.where(me * block < channels, r[:DET], r[DET:])
    dw0 = sum(mine_iw[k][:, None] * mine_r[k][None, :] for k in range(DET))
    grad_conv = jnp.stack([dw0, dw1]).reshape(2, block, 2, width)
    do = gather(jnp.stack([do0, do1]).astype(BF16), n).astype(F32)
    grad_out = jnp.moveaxis(do, 0, 1).reshape(2, width, channels)
    return (grad_input, grad_conv, grad_bias, grad_out)


def solution(mesh):
    in_specs = (
        P(None, ("groups", "seq")),
        P("groups"),
        P(),
        P(),
        P(None, None, None, "tensor"),
        P(None, None, "tensor"),
        P(None, "tensor", None),
        P(("groups", "seq"), None),
    )
    out_specs = (
        P("groups", None),
        P("groups", "seq", None, "tensor"),
        P("groups", None, "tensor"),
        P("groups", "tensor", None),
    )
    return jax.shard_map(body, mesh=mesh, in_specs=in_specs, out_specs=out_specs, check_vma=False)
```

```python
import functools
import math

import jax
import jax.numpy as jnp
from jax import lax
from jax.experimental import pallas as pl
from jax.experimental.pallas import tpu as pltpu
from jax.sharding import PartitionSpec as P

DET = 3
DILATION_EXPONENT = 9
MAXSHIFT = 128
LAG = 2**DILATION_EXPONENT
F32 = jnp.float32
BF16 = jnp.bfloat16
VMEM = pl.BlockSpec(memory_space=pltpu.VMEM)
SMEM = pl.BlockSpec(memory_space=pltpu.SMEM)


def dot(a, b, dims):
    return lax.dot_general(a, b, (dims, ((), ())), preferred_element_type=F32)


def swap(x):
    return lax.ppermute(x, "tensor", [(0, 1), (1, 0)])


def halves(x):
    hi = x.astype(BF16).astype(F32)
    return hi, x - hi


def gates(filt, gate):
    return jnp.tanh(filt), 0.5 * jnp.tanh(0.5 * gate) + 0.5


def taps(x, w, layer, half, rows):
    sl = slice(half * rows, (half + 1) * rows)
    return [dot(x, w[layer, g, sl, :], ((1,), (0,))) for g in range(2)]


def untaps(gl, w, layer, half, rows):
    width = w.shape[3]
    sl = slice(half * rows, (half + 1) * rows)
    return dot(gl[:, :width], w[layer, 0, sl, :], ((1,), (1,))) + dot(
        gl[:, width:], w[layer, 1, sl, :], ((1,), (1,))
    )


def rows8(x):
    return sum(x[i : i + 8] for i in range(0, x.shape[0], 8))


def row_tiles(ext):
    return [(0, LAG)] + [(at, min(512, ext - at)) for at in range(LAG, ext, 512)]


def first_layer(offs, dil, prev, own, iw, w, bias, ow, mine, gate0, fa, fb, st, srow, i3, line, sig):
    rows = own.shape[1]
    channels = iw.shape[1]
    width = ow.shape[1]
    ext = rows + LAG
    full = line.shape[1]
    spare = full - 2 * rows
    line[...] = jnp.zeros_like(line)
    line[0:DET, spare : spare + rows] = prev[...]
    line[0:DET, spare + rows :] = own[...]
    sig[...] = jnp.zeros_like(sig)
    for k in range(DET):
        at = LAG + MAXSHIFT - offs[k]
        for j, start in ((k, at - dil[0]), (DET + k, at)):
            moved = pltpu.roll(line[...], full - start, 1)
            sig[j : j + 1, :] = moved[k : k + 1, :ext]
    s_hi, s_lo = halves(sig[...])
    stack = jnp.concatenate([s_hi, s_lo, s_hi, jnp.zeros_like(s_hi)], axis=0)
    srow[...] = stack[:16].astype(BF16)
    st[...] = stack.T.astype(BF16)

    i_hi, i_lo = halves(iw[...])
    pad2 = jnp.zeros((2, channels), F32)
    pad3 = jnp.zeros((3, channels), F32)
    pad8 = jnp.zeros((8, channels), F32)
    i3[...] = jnp.concatenate(
        [pad3, i_hi, pad2, pad3, i_hi, pad2, pad3, i_lo, pad2, pad8], axis=0
    ).astype(BF16)
    i2 = jnp.concatenate([i_hi, i_lo, pad2, pad8], axis=0).astype(BF16)
    a_lag = jnp.concatenate(taps(i2, w, 0, 0, channels), axis=1)
    a_cur = jnp.concatenate(taps(i2, w, 0, 1, channels), axis=1)
    a0 = jnp.concatenate(
        [a_lag[:DET] + a_lag[DET : 2 * DET], a_cur[:DET] + a_cur[DET : 2 * DET], pad2[:, : 2 * width]], axis=0
    )
    a_hi, a_lo = halves(a0)
    a3 = jnp.concatenate([a_hi, a_hi, a_lo, jnp.zeros_like(a_hi)], axis=0).astype(BF16)
    for at, size in row_tiles(ext):
        sl = slice(at, at + size)
        pre = dot(st[sl, :], a3, ((1,), (0,)))
        th, sg = gates(pre[:, :width] + bias[0, 0:1, :], pre[:, width:] + bias[0, 1:2, :])
        gate = th * sg
        fa[sl, :] = sg - gate * th
        fb[sl, :] = gate - gate * sg
        gate = gate.astype(BF16)
        gate0[sl, :] = gate
        mine[sl, :] = dot(gate, ow[0], ((1,), (0,))).astype(BF16)


def second_layer(
    scale, dil, mine, other, st, i3, w, bias, ow, cot, part, gl1, gate1, joined, bias1, h1, acc, moved, pre, gg
):
    rows, channels = cot.shape
    width = ow.shape[1]
    ext = rows + LAG
    d = dil[1]
    inside = jnp.where(lax.axis_index("seq") == 0, 0.0, 1.0)

    def hidden(i, carry):
        sl = pl.ds(pl.multiple_of(i * 128, 128), 128)
        h = dot(st[sl, :], i3[...], ((1,), (0,)))
        h = h + mine[sl, :].astype(F32) + other[sl, :].astype(F32)
        h1[sl, :] = h * jnp.where(i * 128 < LAG, inside, 1.0)
        return carry

    lax.fori_loop(0, ext // 128, hidden, 0)
    near = LAG - pl.multiple_of((d // 8) * 8, 8)

    @pl.when(d >= 8)
    def _():
        joined[:, :channels] = h1[pl.ds(pl.multiple_of(near, 8), rows), :].astype(BF16)

    @pl.when(d < 8)
    def _():
        joined[:, :channels] = pltpu.roll(h1[LAG - 8 :, :], d, 0)[8:].astype(BF16)

    joined[:, channels:] = h1[LAG:, :].astype(BF16)
    for g in range(2):
        pre[:, g * width : (g + 1) * width] = dot(joined[...], w[1, g], ((1,), (0,)))
    gg[...] = dot(cot[...], ow[1], ((1,), (1,)))

    def local(i, total):
        sl = pl.ds(pl.multiple_of(i * 32, 32), 32)
        th, sg = gates(pre[sl, :width] + bias[1, 0:1, :], pre[sl, width:] + bias[1, 1:2, :])
        gate = th * sg
        gate1[sl, :] = gate.astype(BF16)
        up = gg[sl, :] * scale
        gf = up * (sg - gate * th)
        gs = up * (gate - gate * sg)
        gl1[sl, :width] = gf.astype(BF16)
        gl1[sl, width:] = gs.astype(BF16)
        return total[0] + rows8(gf), total[1] + rows8(gs)

    zero = jnp.zeros((8, width), F32)
    tf, ts = lax.fori_loop(0, rows // 32, local, (zero, zero))
    bias1[:, :width] = jnp.sum(tf, axis=0, keepdims=True)
    bias1[:, width:] = jnp.sum(ts, axis=0, keepdims=True)
    acc[:LAG, :] = jnp.zeros((LAG, channels), F32)
    moved[:8, :] = jnp.zeros((8, channels), F32)
    acc[LAG:, :] = untaps(gl1[...], w, 1, 1, channels)
    moved[8:, :] = untaps(gl1[...], w, 1, 0, channels)

    @pl.when(d >= 8)
    def _():
        acc[pl.ds(pl.multiple_of(near, 8), rows), :] += moved[8:, :]

    @pl.when(d < 8)
    def _():
        acc[LAG - 8 :, :] += pltpu.roll(moved[...], rows + 8 - d, 0)

    part[...] = acc[...].astype(BF16)


def first_back(
    scale, part, apart, cot, gate0, fa, fb, srow, ow, w, bias1, do1, *refs
):
    outs, (adj_s, gl_s, out_s, gg) = refs[:-4], refs[-4:]
    rows, channels = cot.shape
    width = ow.shape[1]
    ext = rows + LAG
    inside = jnp.where(lax.axis_index("seq") == 0, 0.0, 1.0)
    first = jnp.where(lax.axis_index("tensor") == 0, 1.0, 0.0)
    adj_s[:LAG, :] = ((part[:LAG, :].astype(F32) + apart[:LAG, :].astype(F32)) * inside).astype(BF16)
    adj_s[LAG:, :] = (
        part[LAG:, :].astype(F32) + apart[LAG:, :].astype(F32) + cot[...].astype(F32) * scale
    ).astype(BF16)
    gg[...] = dot(adj_s[...], ow[0], ((1,), (1,)))

    def local(i, total):
        sl = pl.ds(pl.multiple_of(i * 64, 64), 64)
        gf = gg[sl, :] * fa[sl, :]
        gs = gg[sl, :] * fb[sl, :]
        gl_s[sl, :width] = gf.astype(BF16)
        gl_s[sl, width:] = gs.astype(BF16)
        return total[0] + rows8(gf), total[1] + rows8(gs)

    zero = jnp.zeros((8, width), F32)
    tf, ts = lax.fori_loop(0, ext // 64, local, (zero, zero))
    bias = jnp.concatenate([jnp.sum(tf, axis=0, keepdims=True), jnp.sum(ts, axis=0, keepdims=True)], axis=1)
    out_s[...] = dot(gate0[...], adj_s[...], ((0,), (0,))).reshape(out_s.shape)
    r2 = dot(srow[...], gl_s[...], ((1,), (0,)))
    g2 = dot(srow[...], adj_s[...], ((1,), (0,)))
    r = r2[:8] + r2[8:]
    g = (g2[:8] + g2[8:]) * first
    r_hi, r_lo = halves(r)
    rr = jnp.concatenate([r_hi, r_lo], axis=0).astype(BF16)
    b_lag = untaps(rr, w, 0, 0, channels)
    b_cur = untaps(rr, w, 0, 1, channels)
    b_lag = b_lag[:8] + b_lag[8:]
    b_cur = b_cur[:8] + b_cur[8:]
    g = g[DET : 2 * DET] + b_lag[:DET] + b_cur[DET : 2 * DET]
    small = jnp.concatenate(
        [r[: 2 * DET], g, bias, bias1[...], jnp.zeros((5, 2 * width), F32)], axis=0
    )
    if len(outs) == 2:
        outs[0][...] = out_s[...].reshape(outs[0].shape)
        outs[1][...] = small
    else:
        m = out_s.shape[1]
        outs[0][:, :m, :] = out_s[...].astype(BF16)
        outs[0][:, m : 2 * m, :] = do1[...].reshape(out_s.shape)
        outs[0][:, 2 * m :, :] = jnp.broadcast_to(small.astype(BF16)[None], (8,) + small.shape)


def out_grad(scale, gate1, cot, out):
    out[...] = (dot(gate1[...], cot[...], ((0,), (0,))) * scale).astype(BF16)


def conv_grad(joined, gl1, keep, send, full):
    x = lax.axis_index("seq") & 1
    full[...] = dot(joined[...], gl1[...], ((0,), (0,))).reshape(full.shape)
    for z in range(4):
        keep[z] = full[2 * z + x]
        send[z] = full[2 * z + 1 - x].astype(BF16)


def pair_add(keep, got, own, send):
    z = lax.axis_index("seq") >> 1
    for k, ref, i in ((0, own, 0), (2, own, 1), (1, send, 0), (3, send, 1)):
        ref[i] = (keep[z ^ k] + got[z ^ k].astype(F32)).astype(ref.dtype)


def pair_add_again(keep, got, own, send):
    own[...] = keep[0] + got[0].astype(F32)
    send[...] = (keep[1] + got[1].astype(F32)).astype(BF16)


def sum_blocks(got, blocks, small):
    m = blocks.shape[1]
    total = got[0].astype(F32)
    for k in range(1, 8):
        total = total + got[k].astype(F32)
    small[...] = total[m:]
    both = total[:m].astype(BF16)
    for k in range(8):
        blocks[k] = both


def scatter_sum(x, n):
    blocks = x.astype(BF16).reshape(n, x.shape[0] // n, x.shape[1])
    got = lax.all_to_all(blocks, "seq", 0, 0, tiled=True)
    return jnp.sum(got.astype(F32), axis=0)


def gather(x, n):
    return lax.all_to_all(jnp.broadcast_to(x[None], (n,) + x.shape), "seq", 0, 0, tiled=True)


def along(x, k):
    n = lax.axis_size("seq")
    return lax.ppermute(x, "seq", [(i, i ^ k) for i in range(n)])


def shape(dims, dtype):
    return jax.ShapeDtypeStruct(dims, dtype)


def all_to_all(x):
    return lax.all_to_all(x, "seq", 0, 0, tiled=True)


def pair_shapes(lead, m, channels):
    dims = (lead, m, channels) if lead else (m, channels)
    return [shape(dims, F32), shape(dims, BF16)]


def limit(mib):
    return pltpu.CompilerParams(vmem_limit_bytes=mib * 2**20)


def call(kernel, out_shape, scratch=()):
    def run(*args):
        count = len(out_shape) if isinstance(out_shape, list) else 0
        return pl.pallas_call(
            kernel,
            out_shape=out_shape,
            in_specs=[VMEM] * len(args),
            out_specs=[VMEM] * count if count else VMEM,
            scratch_shapes=list(scratch),
            compiler_params=limit(8),
            name=getattr(kernel, "func", kernel).__name__,
        )(*args)

    return run


def body(strain, offsets, dilation, input_weight, conv_weight, conv_bias, out_weight, cotangent):
    rows = strain.shape[1]
    channels = input_weight.shape[1]
    width = conv_weight.shape[3]
    n = lax.axis_size("seq")
    me = lax.axis_index("seq")
    ext = LAG + rows
    scale = 1.0 / math.sqrt(rows * n)
    prev = lax.ppermute(strain, "seq", [(i, i + 1) for i in range(n - 1)])
    weight = jnp.transpose(conv_weight, (0, 2, 1, 3))
    full = ext + LAG + MAXSHIFT
    mine, gate0, fa, fb, st, srow, i3 = pl.pallas_call(
        first_layer,
        out_shape=[
            shape((ext, channels), BF16),
            shape((ext, width), BF16),
            shape((ext, width), F32),
            shape((ext, width), F32),
            shape((ext, 32), BF16),
            shape((16, ext), BF16),
            shape((32, channels), BF16),
        ],
        in_specs=[SMEM, SMEM] + [VMEM] * 6,
        out_specs=[VMEM] * 7,
        scratch_shapes=[pltpu.VMEM((8, full), F32), pltpu.VMEM((8, ext), F32)],
        compiler_params=limit(10),
        name="first_layer",
    )(offsets, dilation, prev, strain, input_weight, weight, conv_bias, out_weight)
    other = swap(mine)
    part, gl1, gate1, joined, bias1 = pl.pallas_call(
        functools.partial(second_layer, scale),
        out_shape=[
            shape((ext, channels), BF16),
            shape((rows, 2 * width), BF16),
            shape((rows, width), BF16),
            shape((rows, 2 * channels), BF16),
            shape((1, 2 * width), F32),
        ],
        in_specs=[SMEM] + [VMEM] * 8,
        out_specs=[VMEM] * 5,
        scratch_shapes=[
            pltpu.VMEM((ext, channels), F32),
            pltpu.VMEM((ext, channels), F32),
            pltpu.VMEM((rows + 8, channels), F32),
            pltpu.VMEM((rows, 2 * width), F32),
            pltpu.VMEM((rows, width), F32),
        ],
        compiler_params=limit(28),
        name="second_layer",
    )(dilation, mine, other, st, i3, weight, conv_bias, out_weight, cotangent)
    apart = swap(part)

    if n == 8:
        c_keep, c_send = call(
            conv_grad,
            [shape((4, channels // 4, 2 * width), F32), shape((4, channels // 4, 2 * width), BF16)],
            [pltpu.VMEM((8, channels // 4, 2 * width), F32)],
        )(joined, gl1)
        c_got = along(c_send, 1)
    do1 = call(functools.partial(out_grad, scale), shape((width, channels), BF16))(gate1, cotangent)
    m = width // n
    if n == 8:
        back_shapes = [shape((n, 2 * m + 16, channels), BF16)]
        held = (n, m, channels)
    else:
        back_shapes = [shape((width, channels), F32), shape((16, 2 * width), F32)]
        held = (width, channels)
    back = pl.pallas_call(
        functools.partial(first_back, scale),
        out_shape=back_shapes,
        in_specs=[VMEM] * 11,
        out_specs=[VMEM] * len(back_shapes),
        scratch_shapes=[
            pltpu.VMEM((ext, channels), BF16),
            pltpu.VMEM((ext, 2 * width), BF16),
            pltpu.VMEM(held, F32),
            pltpu.VMEM((ext, width), F32),
        ],
        compiler_params=limit(16),
        name="first_back",
    )(part, apart, cotangent, gate0, fa, fb, srow, out_weight, weight, bias1, do1)
    if n == 8:
        back_got = all_to_all(back[0])
        c_two, c_send = call(pair_add, pair_shapes(2, channels // 4, 2 * width))(c_keep, c_got)
        c_got = along(c_send, 2)
        blocks, small = call(
            sum_blocks, [shape((n, 2 * m, channels), BF16), shape((16, channels), F32)]
        )(back_got)
        do = all_to_all(blocks)
        c_own, c_send = call(pair_add_again, pair_shapes(0, channels // 4, 2 * width))(c_two, c_got)
        c_got = along(c_send, 4)
        dw1 = c_own + c_got.astype(F32)
        do = jnp.transpose(do.reshape(n, 2, m, channels), (1, 0, 2, 3)).astype(F32)
        grad_out = do.reshape(2, width, channels)
    else:
        dw1 = scatter_sum(dot(joined, gl1, ((0,), (0,))), n)
        do1 = scatter_sum(do1, n)
        do0 = scatter_sum(back[0], n)
        small = jnp.sum(gather(back[1], n), axis=0)
        do = gather(jnp.stack([do0, do1]).astype(BF16), n).astype(F32)
        grad_out = jnp.moveaxis(do, 0, 1).reshape(2, width, channels)
    r, g, bias = small[: 2 * DET], small[2 * DET : 3 * DET], small[3 * DET : 3 * DET + 2]
    grad_input = g + swap(g)
    grad_bias = bias.reshape(2, 2, width)
    block = 2 * channels // n
    mine_iw = lax.dynamic_slice_in_dim(input_weight, (me * block) % channels, block, 1)
    mine_r = jnp.where(me * block < channels, r[:DET], r[DET:])
    dw0 = sum(mine_iw[k][:, None] * mine_r[k][None, :] for k in range(DET))
    grad_conv = jnp.stack([dw0, dw1]).reshape(2, block, 2, width)
    return (grad_input, grad_conv, grad_bias, grad_out)


def solution(mesh):
    in_specs = (
        P(None, ("groups", "seq")),
        P("groups"),
        P(),
        P(),
        P(None, None, None, "tensor"),
        P(None, None, "tensor"),
        P(None, "tensor", None),
        P(("groups", "seq"), None),
    )
    out_specs = (
        P("groups", None),
        P("groups", "seq", None, "tensor"),
        P("groups", None, "tensor"),
        P("groups", "tensor", None),
    )
    return jax.shard_map(body, mesh=mesh, in_specs=in_specs, out_specs=out_specs, check_vma=False)
```

```python
import functools
import math

import jax
import jax.numpy as jnp
from jax import lax
from jax.experimental import pallas as pl
from jax.experimental.pallas import tpu as pltpu
from jax.sharding import PartitionSpec as P

DET = 3
DILATION_EXPONENT = 9
MAXSHIFT = 128
LAG = 2**DILATION_EXPONENT
F32 = jnp.float32
BF16 = jnp.bfloat16
VMEM = pl.BlockSpec(memory_space=pltpu.VMEM)
SMEM = pl.BlockSpec(memory_space=pltpu.SMEM)


def dot(a, b, dims):
    return lax.dot_general(a, b, (dims, ((), ())), preferred_element_type=F32)


def swap(x):
    return lax.ppermute(x, "tensor", [(0, 1), (1, 0)])


def halves(x):
    hi = x.astype(BF16).astype(F32)
    return hi, x - hi


def gates(filt, gate):
    return jnp.tanh(filt), 0.5 * jnp.tanh(0.5 * gate) + 0.5


def taps(x, w, layer, half, rows):
    sl = slice(half * rows, (half + 1) * rows)
    return [dot(x, w[layer, g, sl, :], ((1,), (0,))) for g in range(2)]


def untaps(gl, w, layer, half, rows):
    width = w.shape[3]
    sl = slice(half * rows, (half + 1) * rows)
    return dot(gl[:, :width], w[layer, 0, sl, :], ((1,), (1,))) + dot(
        gl[:, width:], w[layer, 1, sl, :], ((1,), (1,))
    )


def rows8(x):
    return sum(x[i : i + 8] for i in range(0, x.shape[0], 8))


def row_tiles(ext):
    return [(0, LAG)] + [(at, min(512, ext - at)) for at in range(LAG, ext, 512)]


def first_layer(offs, dil, prev, own, iw, w, bias, ow, mine, gate0, fa, fb, st, srow, i3, line, sig):
    rows = own.shape[1]
    channels = iw.shape[1]
    width = ow.shape[1]
    ext = rows + LAG
    full = line.shape[1]
    spare = full - 2 * rows
    line[...] = jnp.zeros_like(line)
    line[0:DET, spare : spare + rows] = prev[...]
    line[0:DET, spare + rows :] = own[...]
    sig[...] = jnp.zeros_like(sig)
    for k in range(DET):
        at = LAG + MAXSHIFT - offs[k]
        for j, start in ((k, at - dil[0]), (DET + k, at)):
            moved = pltpu.roll(line[...], full - start, 1)
            sig[j : j + 1, :] = moved[k : k + 1, :ext]
    s_hi, s_lo = halves(sig[...])
    stack = jnp.concatenate([s_hi, s_lo, s_hi, jnp.zeros_like(s_hi)], axis=0)
    srow[...] = stack[:16].astype(BF16)
    st[...] = stack.T.astype(BF16)

    i_hi, i_lo = halves(iw[...])
    pad2 = jnp.zeros((2, channels), F32)
    pad3 = jnp.zeros((3, channels), F32)
    pad8 = jnp.zeros((8, channels), F32)
    i3[...] = jnp.concatenate(
        [pad3, i_hi, pad2, pad3, i_hi, pad2, pad3, i_lo, pad2, pad8], axis=0
    ).astype(BF16)
    i2 = jnp.concatenate([i_hi, i_lo, pad2, pad8], axis=0).astype(BF16)
    a_lag = jnp.concatenate(taps(i2, w, 0, 0, channels), axis=1)
    a_cur = jnp.concatenate(taps(i2, w, 0, 1, channels), axis=1)
    a0 = jnp.concatenate(
        [a_lag[:DET] + a_lag[DET : 2 * DET], a_cur[:DET] + a_cur[DET : 2 * DET], pad2[:, : 2 * width]], axis=0
    )
    a_hi, a_lo = halves(a0)
    a3 = jnp.concatenate([a_hi, a_hi, a_lo, jnp.zeros_like(a_hi)], axis=0).astype(BF16)
    for at, size in row_tiles(ext):
        sl = slice(at, at + size)
        pre = dot(st[sl, :], a3, ((1,), (0,)))
        th, sg = gates(pre[:, :width] + bias[0, 0:1, :], pre[:, width:] + bias[0, 1:2, :])
        gate = th * sg
        fa[sl, :] = sg - gate * th
        fb[sl, :] = gate - gate * sg
        gate = gate.astype(BF16)
        gate0[sl, :] = gate
        mine[sl, :] = dot(gate, ow[0], ((1,), (0,))).astype(BF16)


def second_layer(
    scale, dil, mine, other, st, i3, w, bias, ow, cot, part, gl1, gate1, joined, bias1, h1, acc, moved, pre, gg
):
    rows, channels = cot.shape
    width = ow.shape[1]
    ext = rows + LAG
    d = dil[1]
    inside = jnp.where(lax.axis_index("seq") == 0, 0.0, 1.0)

    h1[...] = dot(st[...], i3[...], ((1,), (0,)))
    h1[:LAG, :] = (h1[:LAG, :] + mine[:LAG, :].astype(F32) + other[:LAG, :].astype(F32)) * inside
    h1[LAG:, :] = h1[LAG:, :] + mine[LAG:, :].astype(F32) + other[LAG:, :].astype(F32)
    near = LAG - pl.multiple_of((d // 8) * 8, 8)

    @pl.when(d >= 8)
    def _():
        joined[:, :channels] = h1[pl.ds(pl.multiple_of(near, 8), rows), :].astype(BF16)

    @pl.when(d < 8)
    def _():
        def step(i, carry):
            at = pl.multiple_of(i * 64, 64)
            x = h1[pl.ds(pl.multiple_of(LAG - 8 + at, 8), 72), :]
            joined[pl.ds(at, 64), :channels] = pltpu.roll(x, d, 0)[8:].astype(BF16)
            return carry

        lax.fori_loop(0, rows // 64, step, 0)

    joined[:, channels:] = h1[LAG:, :].astype(BF16)
    for g in range(2):
        pre[:, g * width : (g + 1) * width] = dot(joined[...], w[1, g], ((1,), (0,)))
    gg[...] = dot(cot[...], ow[1], ((1,), (1,)))

    def local(i, total):
        sl = pl.ds(pl.multiple_of(i * 32, 32), 32)
        th, sg = gates(pre[sl, :width] + bias[1, 0:1, :], pre[sl, width:] + bias[1, 1:2, :])
        gate = th * sg
        gate1[sl, :] = gate.astype(BF16)
        up = gg[sl, :] * scale
        gf = up * (sg - gate * th)
        gs = up * (gate - gate * sg)
        gl1[sl, :width] = gf.astype(BF16)
        gl1[sl, width:] = gs.astype(BF16)
        return total[0] + rows8(gf), total[1] + rows8(gs)

    zero = jnp.zeros((8, width), F32)
    tf, ts = lax.fori_loop(0, rows // 32, local, (zero, zero), unroll=4)
    bias1[:, :width] = jnp.sum(tf, axis=0, keepdims=True)
    bias1[:, width:] = jnp.sum(ts, axis=0, keepdims=True)
    acc[:LAG, :] = jnp.zeros((LAG, channels), F32)
    moved[:8, :] = jnp.zeros((8, channels), F32)
    moved[rows + 8 :, :] = jnp.zeros((8, channels), F32)
    acc[LAG:, :] = untaps(gl1[...], w, 1, 1, channels)
    moved[8 : rows + 8, :] = untaps(gl1[...], w, 1, 0, channels)

    @pl.when(d >= 8)
    def _():
        acc[pl.ds(pl.multiple_of(near, 8), rows), :] += moved[8 : rows + 8, :]

    @pl.when(d < 8)
    def _():
        def step(i, carry):
            at = pl.multiple_of(i * 64, 64)
            x = pltpu.roll(moved[pl.ds(at, 72), :], 72 - d, 0)[:64]
            acc[pl.ds(pl.multiple_of(LAG - 8 + at, 8), 64), :] += x
            return carry

        lax.fori_loop(0, rows // 64, step, 0)
        acc[ext - 8 :, :] += pltpu.roll(moved[rows:, :], 16 - d, 0)[:8]

    part[...] = acc[...].astype(BF16)


def first_back(
    scale, part, apart, cot, gate0, fa, fb, srow, ow, w, bias1, do1, *refs
):
    outs, (adj_s, gl_s, out_s, gg) = refs[:-4], refs[-4:]
    rows, channels = cot.shape
    width = ow.shape[1]
    ext = rows + LAG
    inside = jnp.where(lax.axis_index("seq") == 0, 0.0, 1.0)
    first = jnp.where(lax.axis_index("tensor") == 0, 1.0, 0.0)
    adj_s[:LAG, :] = ((part[:LAG, :].astype(F32) + apart[:LAG, :].astype(F32)) * inside).astype(BF16)
    adj_s[LAG:, :] = (
        part[LAG:, :].astype(F32) + apart[LAG:, :].astype(F32) + cot[...].astype(F32) * scale
    ).astype(BF16)
    gg[...] = dot(adj_s[...], ow[0], ((1,), (1,)))

    def local(i, total):
        sl = pl.ds(pl.multiple_of(i * 64, 64), 64)
        gf = gg[sl, :] * fa[sl, :]
        gs = gg[sl, :] * fb[sl, :]
        gl_s[sl, :width] = gf.astype(BF16)
        gl_s[sl, width:] = gs.astype(BF16)
        return total[0] + rows8(gf), total[1] + rows8(gs)

    zero = jnp.zeros((8, width), F32)
    tf, ts = lax.fori_loop(0, ext // 64, local, (zero, zero), unroll=2)
    bias = jnp.concatenate([jnp.sum(tf, axis=0, keepdims=True), jnp.sum(ts, axis=0, keepdims=True)], axis=1)
    out_s[...] = dot(gate0[...], adj_s[...], ((0,), (0,))).reshape(out_s.shape)
    r2 = dot(srow[...], gl_s[...], ((1,), (0,)))
    g2 = dot(srow[...], adj_s[...], ((1,), (0,)))
    r = r2[:8] + r2[8:]
    g = (g2[:8] + g2[8:]) * first
    r_hi, r_lo = halves(r)
    rr = jnp.concatenate([r_hi, r_lo], axis=0).astype(BF16)
    b_lag = untaps(rr, w, 0, 0, channels)
    b_cur = untaps(rr, w, 0, 1, channels)
    b_lag = b_lag[:8] + b_lag[8:]
    b_cur = b_cur[:8] + b_cur[8:]
    g = g[DET : 2 * DET] + b_lag[:DET] + b_cur[DET : 2 * DET]
    small = jnp.concatenate(
        [r[: 2 * DET], g, bias, bias1[...], jnp.zeros((5, 2 * width), F32)], axis=0
    )
    if len(outs) == 2:
        outs[0][...] = out_s[...].reshape(outs[0].shape)
        outs[1][...] = small
    else:
        m = out_s.shape[1]
        z = lax.axis_index("seq") >> 1
        for k in range(4):
            outs[k][:m, :] = out_s[z ^ k].astype(BF16)
            outs[k][m : 2 * m, :] = do1[pl.ds(pl.multiple_of((z ^ k) * m, m), m), :]
            outs[k][2 * m :, :] = small.astype(BF16)


def out_grad(scale, gate1, cot, out):
    out[...] = (dot(gate1[...], cot[...], ((0,), (0,))) * scale).astype(BF16)


def conv_grad(joined, gl1, keep, send, full):
    x = lax.axis_index("seq") & 1
    full[...] = dot(joined[...], gl1[...], ((0,), (0,))).reshape(full.shape)
    for z in range(4):
        keep[z] = full[2 * z + x]
        send[z] = full[2 * z + 1 - x].astype(BF16)


def pair_add(keep, got, own, send):
    z = lax.axis_index("seq") >> 1
    for k, ref, i in ((0, own, 0), (2, own, 1), (1, send, 0), (3, send, 1)):
        ref[i] = (keep[z ^ k] + got[z ^ k].astype(F32)).astype(ref.dtype)


def pair_add_again(keep, got, own, send):
    own[...] = keep[0] + got[0].astype(F32)
    send[...] = (keep[1] + got[1].astype(F32)).astype(BF16)


def quarter_sum(own, r1, r2, r3, total, held):
    z = lax.axis_index("seq") >> 1
    for k, ref in enumerate((own, r1, r2, r3)):
        held[z ^ k] = ref[...].astype(F32)
    total[...] = (held[0] + held[1] + held[2] + held[3]).astype(BF16)


def half_sum(own, got, blocks, small):
    m = blocks.shape[0]
    total = own[...].astype(F32) + got[...].astype(F32)
    blocks[...] = total[:m].astype(BF16)
    small[...] = total[m:]


def first_conv(iw, small, out):
    me = lax.axis_index("seq")
    block, channels = out.shape[0], iw.shape[1]
    at = pl.multiple_of((me & 3) * block, block)
    i_hi, i_lo = halves(iw[:, pl.ds(at, block)])
    r_hi, r_lo = halves(jnp.where(me < 4, small[:DET, :], small[DET : 2 * DET, :]))
    left = jnp.concatenate([i_hi, i_lo, i_hi, jnp.zeros((7, block), F32)], axis=0).astype(BF16)
    right = jnp.concatenate([r_hi, r_hi, r_lo, jnp.zeros((7, channels), F32)], axis=0).astype(BF16)
    out[...] = dot(left, right, ((0,), (0,)))


def finish(own, r1, r2, r3, out):
    z = lax.axis_index("seq") >> 1
    m = own.shape[0] // 2
    for k, ref in enumerate((own, r1, r2, r3)):
        for layer in range(2):
            out[layer, pl.ds(pl.multiple_of((z ^ k) * m, m), m), :] = ref[layer * m : (layer + 1) * m, :].astype(F32)


def scatter_sum(x, n):
    blocks = x.astype(BF16).reshape(n, x.shape[0] // n, x.shape[1])
    got = lax.all_to_all(blocks, "seq", 0, 0, tiled=True)
    return jnp.sum(got.astype(F32), axis=0)


def gather(x, n):
    return lax.all_to_all(jnp.broadcast_to(x[None], (n,) + x.shape), "seq", 0, 0, tiled=True)


def along(x, k):
    n = lax.axis_size("seq")
    return lax.ppermute(x, "seq", [(i, i ^ k) for i in range(n)])


def shape(dims, dtype):
    return jax.ShapeDtypeStruct(dims, dtype)


def all_to_all(x):
    return lax.all_to_all(x, "seq", 0, 0, tiled=True)


def pair_shapes(lead, m, channels):
    dims = (lead, m, channels) if lead else (m, channels)
    return [shape(dims, F32), shape(dims, BF16)]


def limit(mib):
    return pltpu.CompilerParams(vmem_limit_bytes=mib * 2**20)


def after(x, y):
    return lax.optimization_barrier((x, y))[0]


def cost(us):
    return pl.CostEstimate(flops=int(us * 8e8), bytes_accessed=int(us * 3e6), transcendentals=0)


def call(kernel, out_shape, scratch=(), us=1.0):
    def run(*args):
        count = len(out_shape) if isinstance(out_shape, list) else 0
        return pl.pallas_call(
            kernel,
            out_shape=out_shape,
            in_specs=[VMEM] * len(args),
            out_specs=[VMEM] * count if count else VMEM,
            scratch_shapes=list(scratch),
            compiler_params=limit(8),
            cost_estimate=cost(us),
            name=getattr(kernel, "func", kernel).__name__,
        )(*args)

    return run


def body(strain, offsets, dilation, input_weight, conv_weight, conv_bias, out_weight, cotangent):
    rows = strain.shape[1]
    channels = input_weight.shape[1]
    width = conv_weight.shape[3]
    n = lax.axis_size("seq")
    me = lax.axis_index("seq")
    ext = LAG + rows
    scale = 1.0 / math.sqrt(rows * n)
    prev = lax.ppermute(strain, "seq", [(i, i + 1) for i in range(n - 1)])
    weight = jnp.transpose(conv_weight, (0, 2, 1, 3))
    full = ext + LAG + MAXSHIFT
    mine, gate0, fa, fb, st, srow, i3 = pl.pallas_call(
        first_layer,
        out_shape=[
            shape((ext, channels), BF16),
            shape((ext, width), BF16),
            shape((ext, width), F32),
            shape((ext, width), F32),
            shape((ext, 32), BF16),
            shape((16, ext), BF16),
            shape((32, channels), BF16),
        ],
        in_specs=[SMEM, SMEM] + [VMEM] * 6,
        out_specs=[VMEM] * 7,
        scratch_shapes=[pltpu.VMEM((8, full), F32), pltpu.VMEM((8, ext), F32)],
        compiler_params=limit(10),
        cost_estimate=cost(2),
        name="first_layer",
    )(offsets, dilation, prev, strain, input_weight, weight, conv_bias, out_weight)
    other = swap(mine)
    part, gl1, gate1, joined, bias1 = pl.pallas_call(
        functools.partial(second_layer, scale),
        out_shape=[
            shape((ext, channels), BF16),
            shape((rows, 2 * width), BF16),
            shape((rows, width), BF16),
            shape((rows, 2 * channels), BF16),
            shape((1, 2 * width), F32),
        ],
        in_specs=[SMEM] + [VMEM] * 8,
        out_specs=[VMEM] * 5,
        scratch_shapes=[
            pltpu.VMEM((ext, channels), F32),
            pltpu.VMEM((ext, channels), F32),
            pltpu.VMEM((rows + 16, channels), F32),
            pltpu.VMEM((rows, 2 * width), F32),
            pltpu.VMEM((rows, width), F32),
        ],
        compiler_params=limit(28),
        cost_estimate=cost(7),
        name="second_layer",
    )(dilation, mine, other, st, i3, weight, conv_bias, out_weight, cotangent)
    apart = swap(part)

    if n == 8:
        c_keep, c_send = call(
            conv_grad,
            [shape((4, channels // 4, 2 * width), F32), shape((4, channels // 4, 2 * width), BF16)],
            [pltpu.VMEM((8, channels // 4, 2 * width), F32)],
            1.5,
        )(joined, gl1)
        c_got = along(c_send, 1)
        apart = after(apart, c_send)
    do1 = call(functools.partial(out_grad, scale), shape((width, channels), BF16))(gate1, cotangent)
    m = width // n
    if n == 8:
        m = width // 4
        back_shapes = [shape((2 * m + 16, channels), BF16)] * 4
        held = (4, m, channels)
    else:
        back_shapes = [shape((width, channels), F32), shape((16, 2 * width), F32)]
        held = (width, channels)
    back = pl.pallas_call(
        functools.partial(first_back, scale),
        out_shape=back_shapes,
        in_specs=[VMEM] * 11,
        out_specs=[VMEM] * len(back_shapes),
        scratch_shapes=[
            pltpu.VMEM((ext, channels), BF16),
            pltpu.VMEM((ext, 2 * width), BF16),
            pltpu.VMEM(held, F32),
            pltpu.VMEM((ext, width), F32),
        ],
        compiler_params=limit(16),
        cost_estimate=cost(4),
        name="first_back",
    )(part, apart, cotangent, gate0, fa, fb, srow, out_weight, weight, bias1, do1)
    if n == 8:
        got = [along(back[k], 2 * k) for k in (1, 2, 3)]
        c_keep = after(c_keep, back[0])
        c_two, c_send = call(pair_add, pair_shapes(2, channels // 4, 2 * width))(c_keep, c_got)
        c_got = along(c_send, 2)
        quarter = call(quarter_sum, shape(back[0].shape, BF16), [pltpu.VMEM((4,) + back[0].shape, F32)])(back[0], *got)
        other = along(quarter, 1)
        c_own, c_send = call(pair_add_again, pair_shapes(0, channels // 4, 2 * width))(c_two, c_got)
        c_got = along(c_send, 4)
        blocks, small = call(half_sum, [shape((2 * m, channels), BF16), shape((16, channels), F32)])(quarter, other)
        got = [along(blocks, 2 * k) for k in (1, 2, 3)]
        dw1 = c_own + c_got.astype(F32)
        grad_out = call(finish, shape((2, width, channels), F32))(blocks, *got)
    else:
        dw1 = scatter_sum(dot(joined, gl1, ((0,), (0,))), n)
        do1 = scatter_sum(do1, n)
        do0 = scatter_sum(back[0], n)
        small = jnp.sum(gather(back[1], n), axis=0)
        do = gather(jnp.stack([do0, do1]).astype(BF16), n).astype(F32)
        grad_out = jnp.moveaxis(do, 0, 1).reshape(2, width, channels)
    r, g, bias = small[: 2 * DET], small[2 * DET : 3 * DET], small[3 * DET : 3 * DET + 2]
    grad_input = g + swap(g)
    grad_bias = bias.reshape(2, 2, width)
    block = 2 * channels // n
    if n == 8:
        dw0 = call(first_conv, shape((block, 2 * width), F32))(input_weight, small)
    else:
        mine_iw = lax.dynamic_slice_in_dim(input_weight, (me * block) % channels, block, 1)
        mine_r = jnp.where(me * block < channels, r[:DET], r[DET:])
        dw0 = sum(mine_iw[k][:, None] * mine_r[k][None, :] for k in range(DET))
    grad_conv = jnp.stack([dw0, dw1]).reshape(2, block, 2, width)
    return (grad_input, grad_conv, grad_bias, grad_out)


def solution(mesh):
    in_specs = (
        P(None, ("groups", "seq")),
        P("groups"),
        P(),
        P(),
        P(None, None, None, "tensor"),
        P(None, None, "tensor"),
        P(None, "tensor", None),
        P(("groups", "seq"), None),
    )
    out_specs = (
        P("groups", None),
        P("groups", "seq", None, "tensor"),
        P("groups", None, "tensor"),
        P("groups", "tensor", None),
    )
    return jax.shard_map(body, mesh=mesh, in_specs=in_specs, out_specs=out_specs, check_vma=False)
```

```python
import functools
import math

import jax
import jax.numpy as jnp
from jax import lax
from jax.experimental import pallas as pl
from jax.experimental.pallas import tpu as pltpu
from jax.sharding import PartitionSpec as P

DET = 3
DILATION_EXPONENT = 9
MAXSHIFT = 128
LAG = 2**DILATION_EXPONENT
F32 = jnp.float32
BF16 = jnp.bfloat16
VMEM = pl.BlockSpec(memory_space=pltpu.VMEM)
SMEM = pl.BlockSpec(memory_space=pltpu.SMEM)


def dot(a, b, dims):
    return lax.dot_general(a, b, (dims, ((), ())), preferred_element_type=F32)


def swap(x):
    return lax.ppermute(x, "tensor", [(0, 1), (1, 0)])


def halves(x):
    hi = x.astype(BF16).astype(F32)
    return hi, x - hi


def gates(filt, gate):
    return jnp.tanh(filt), 0.5 * jnp.tanh(0.5 * gate) + 0.5


def taps(x, w, layer, half, rows):
    sl = slice(half * rows, (half + 1) * rows)
    return [dot(x, w[layer, g, sl, :], ((1,), (0,))) for g in range(2)]


def untaps(gl, w, layer, half, rows):
    width = w.shape[3]
    sl = slice(half * rows, (half + 1) * rows)
    return dot(gl[:, :width], w[layer, 0, sl, :], ((1,), (1,))) + dot(
        gl[:, width:], w[layer, 1, sl, :], ((1,), (1,))
    )


def rows8(x):
    return sum(x[i : i + 8] for i in range(0, x.shape[0], 8))


def row_tiles(ext):
    return [(0, LAG)] + [(at, min(512, ext - at)) for at in range(LAG, ext, 512)]


def first_layer(offs, dil, prev, own, iw, w, bias, gate0, fa, fb, st, srow, i3, line, sig):
    rows = own.shape[1]
    channels = iw.shape[1]
    width = w.shape[3]
    ext = rows + LAG
    full = line.shape[1]
    spare = full - 2 * rows
    line[...] = jnp.zeros_like(line)
    line[0:DET, spare : spare + rows] = prev[...]
    line[0:DET, spare + rows :] = own[...]
    sig[...] = jnp.zeros_like(sig)
    for k in range(DET):
        at = LAG + MAXSHIFT - offs[k]
        for j, start in ((k, at - dil[0]), (DET + k, at)):
            moved = pltpu.roll(line[...], full - start, 1)
            sig[j : j + 1, :] = moved[k : k + 1, :ext]
    s_hi, s_lo = halves(sig[...])
    stack = jnp.concatenate([s_hi, s_lo, s_hi, jnp.zeros_like(s_hi)], axis=0)
    srow[...] = stack[:16].astype(BF16)
    st[...] = stack.T.astype(BF16)

    i_hi, i_lo = halves(iw[...])
    pad2 = jnp.zeros((2, channels), F32)
    pad3 = jnp.zeros((3, channels), F32)
    pad8 = jnp.zeros((8, channels), F32)
    i3[...] = jnp.concatenate(
        [pad3, i_hi, pad2, pad3, i_hi, pad2, pad3, i_lo, pad2, pad8], axis=0
    ).astype(BF16)
    i2 = jnp.concatenate([i_hi, i_lo, pad2, pad8], axis=0).astype(BF16)
    a_lag = jnp.concatenate(taps(i2, w, 0, 0, channels), axis=1)
    a_cur = jnp.concatenate(taps(i2, w, 0, 1, channels), axis=1)
    a0 = jnp.concatenate(
        [a_lag[:DET] + a_lag[DET : 2 * DET], a_cur[:DET] + a_cur[DET : 2 * DET], pad2[:, : 2 * width]], axis=0
    )
    a_hi, a_lo = halves(a0)
    a3 = jnp.concatenate([a_hi, a_hi, a_lo, jnp.zeros_like(a_hi)], axis=0).astype(BF16)
    for at, size in row_tiles(ext):
        sl = slice(at, at + size)
        pre = dot(st[sl, :], a3, ((1,), (0,)))
        th, sg = gates(pre[:, :width] + bias[0, 0:1, :], pre[:, width:] + bias[0, 1:2, :])
        gate = th * sg
        fa[sl, :] = sg - gate * th
        fb[sl, :] = gate - gate * sg
        gate0[sl, :] = gate.astype(BF16)


def own_mix(scale, st, i3, gate0, ow, cot, hm, gg):
    hm[...] = dot(st[...], i3[...], ((1,), (0,))) + dot(gate0[...], ow[0], ((1,), (0,)))
    gg[...] = dot(cot[...], ow[1], ((1,), (1,))) * scale


def second_layer(
    dil, hm, gg, gate_far, ow_far, w, bias, part, gl1, gate1, joined, bias1, h1, acc, moved, pre
):
    rows, width = gg.shape
    channels = hm.shape[1]
    ext = rows + LAG
    d = dil[1]
    inside = jnp.where(lax.axis_index("seq") == 0, 0.0, 1.0)

    h1[...] = hm[...] + dot(gate_far[...], ow_far[...], ((1,), (0,)))
    h1[:LAG, :] = h1[:LAG, :] * inside
    near = LAG - pl.multiple_of((d // 8) * 8, 8)

    @pl.when(d >= 8)
    def _():
        joined[:, :channels] = h1[pl.ds(pl.multiple_of(near, 8), rows), :].astype(BF16)

    @pl.when(d < 8)
    def _():
        def step(i, carry):
            at = pl.multiple_of(i * 64, 64)
            x = h1[pl.ds(pl.multiple_of(LAG - 8 + at, 8), 72), :]
            joined[pl.ds(at, 64), :channels] = pltpu.roll(x, d, 0)[8:].astype(BF16)
            return carry

        lax.fori_loop(0, rows // 64, step, 0)

    joined[:, channels:] = h1[LAG:, :].astype(BF16)
    for g in range(2):
        pre[:, g * width : (g + 1) * width] = dot(joined[...], w[1, g], ((1,), (0,)))

    def local(i, total):
        sl = pl.ds(pl.multiple_of(i * 32, 32), 32)
        th, sg = gates(pre[sl, :width] + bias[1, 0:1, :], pre[sl, width:] + bias[1, 1:2, :])
        gate = th * sg
        gate1[sl, :] = gate.astype(BF16)
        up = gg[sl, :]
        gf = up * (sg - gate * th)
        gs = up * (gate - gate * sg)
        gl1[sl, :width] = gf.astype(BF16)
        gl1[sl, width:] = gs.astype(BF16)
        return total[0] + rows8(gf), total[1] + rows8(gs)

    zero = jnp.zeros((8, width), F32)
    tf, ts = lax.fori_loop(0, rows // 32, local, (zero, zero), unroll=4)
    bias1[:, :width] = jnp.sum(tf, axis=0, keepdims=True)
    bias1[:, width:] = jnp.sum(ts, axis=0, keepdims=True)
    acc[:LAG, :] = jnp.zeros((LAG, channels), F32)
    moved[:8, :] = jnp.zeros((8, channels), F32)
    moved[rows + 8 :, :] = jnp.zeros((8, channels), F32)
    acc[LAG:, :] = untaps(gl1[...], w, 1, 1, channels)
    moved[8 : rows + 8, :] = untaps(gl1[...], w, 1, 0, channels)

    @pl.when(d >= 8)
    def _():
        acc[pl.ds(pl.multiple_of(near, 8), rows), :] += moved[8 : rows + 8, :]

    @pl.when(d < 8)
    def _():
        def step(i, carry):
            at = pl.multiple_of(i * 64, 64)
            x = pltpu.roll(moved[pl.ds(at, 72), :], 72 - d, 0)[:64]
            acc[pl.ds(pl.multiple_of(LAG - 8 + at, 8), 64), :] += x
            return carry

        lax.fori_loop(0, rows // 64, step, 0)
        acc[ext - 8 :, :] += pltpu.roll(moved[rows:, :], 16 - d, 0)[:8]

    part[...] = acc[...].astype(BF16)


def first_back(
    scale, part, apart, cot, gate0, fa, fb, srow, ow, w, bias1, out, small, adj_s, gl_s, gg
):
    rows, channels = cot.shape
    width = ow.shape[1]
    ext = rows + LAG
    inside = jnp.where(lax.axis_index("seq") == 0, 0.0, 1.0)
    first = jnp.where(lax.axis_index("tensor") == 0, 1.0, 0.0)
    adj_s[:LAG, :] = ((part[:LAG, :].astype(F32) + apart[:LAG, :].astype(F32)) * inside).astype(BF16)
    adj_s[LAG:, :] = (
        part[LAG:, :].astype(F32) + apart[LAG:, :].astype(F32) + cot[...].astype(F32) * scale
    ).astype(BF16)
    gg[...] = dot(adj_s[...], ow[0], ((1,), (1,)))

    def local(i, total):
        sl = pl.ds(pl.multiple_of(i * 64, 64), 64)
        gf = gg[sl, :] * fa[sl, :]
        gs = gg[sl, :] * fb[sl, :]
        gl_s[sl, :width] = gf.astype(BF16)
        gl_s[sl, width:] = gs.astype(BF16)
        return total[0] + rows8(gf), total[1] + rows8(gs)

    zero = jnp.zeros((8, width), F32)
    tf, ts = lax.fori_loop(0, ext // 64, local, (zero, zero), unroll=2)
    bias = jnp.concatenate([jnp.sum(tf, axis=0, keepdims=True), jnp.sum(ts, axis=0, keepdims=True)], axis=1)
    out[...] = dot(gate0[...], adj_s[...], ((0,), (0,))).astype(BF16)
    r2 = dot(srow[...], gl_s[...], ((1,), (0,)))
    g2 = dot(srow[...], adj_s[...], ((1,), (0,)))
    r = r2[:8] + r2[8:]
    g = (g2[:8] + g2[8:]) * first
    r_hi, r_lo = halves(r)
    rr = jnp.concatenate([r_hi, r_lo], axis=0).astype(BF16)
    b_lag = untaps(rr, w, 0, 0, channels)
    b_cur = untaps(rr, w, 0, 1, channels)
    b_lag = b_lag[:8] + b_lag[8:]
    b_cur = b_cur[:8] + b_cur[8:]
    g = g[DET : 2 * DET] + b_lag[:DET] + b_cur[DET : 2 * DET]
    small[...] = jnp.concatenate(
        [r[: 2 * DET], g, bias, bias1[...], jnp.zeros((5, 2 * width), F32)], axis=0
    )


def pack(out, small, keep, got, *sends):
    z = lax.axis_index("seq") >> 1
    m = out.shape[0] // 4
    h = m // 2
    for k, send in enumerate(sends):
        send[:m, :] = out[pl.ds(pl.multiple_of((z ^ k) * m, m), m), :]
        send[m : m + h, :] = (keep[z ^ k] + got[z ^ k].astype(F32)).astype(BF16)
        send[m + h :, :] = small[...].astype(BF16)


def out_grad(scale, gate1, cot, keep, send, full):
    x = lax.axis_index("seq") & 1
    full[...] = (dot(gate1[...], cot[...], ((0,), (0,))) * scale).reshape(full.shape)
    for z in range(4):
        keep[z] = full[2 * z + x]
        send[z] = full[2 * z + 1 - x].astype(BF16)


def conv_grad(joined, gl1, keep, send, full):
    x = lax.axis_index("seq") & 1
    full[...] = dot(joined[...], gl1[...], ((0,), (0,))).reshape(full.shape)
    for z in range(4):
        keep[z] = full[2 * z + x]
        send[z] = full[2 * z + 1 - x].astype(BF16)


def pair_add(keep, got, own, send):
    z = lax.axis_index("seq") >> 1
    for k, ref, i in ((0, own, 0), (2, own, 1), (1, send, 0), (3, send, 1)):
        ref[i] = (keep[z ^ k] + got[z ^ k].astype(F32)).astype(ref.dtype)


def pair_add_again(keep, got, own, send):
    own[...] = keep[0] + got[0].astype(F32)
    send[...] = (keep[1] + got[1].astype(F32)).astype(BF16)


def quarter_sum(own, r1, r2, r3, total, held):
    z = lax.axis_index("seq") >> 1
    for k, ref in enumerate((own, r1, r2, r3)):
        held[z ^ k] = ref[...].astype(F32)
    total[...] = (held[0] + held[1] + held[2] + held[3]).astype(BF16)


def half_sum(own, got, blocks, small):
    x = lax.axis_index("seq") & 1
    m = blocks.shape[0] // 2
    h = m // 2
    blocks[:m, :] = (own[:m, :].astype(F32) + got[:m, :].astype(F32)).astype(BF16)
    blocks[pl.ds(pl.multiple_of(m + x * h, h), h), :] = own[m : m + h, :]
    blocks[pl.ds(pl.multiple_of(m + (1 - x) * h, h), h), :] = got[m : m + h, :]
    small[...] = own[m + h :, :].astype(F32) + got[m + h :, :].astype(F32)


def first_conv(iw, small, out):
    me = lax.axis_index("seq")
    block, channels = out.shape[0], iw.shape[1]
    at = pl.multiple_of((me & 3) * block, block)
    i_hi, i_lo = halves(iw[:, pl.ds(at, block)])
    r_hi, r_lo = halves(jnp.where(me < 4, small[:DET, :], small[DET : 2 * DET, :]))
    left = jnp.concatenate([i_hi, i_lo, i_hi, jnp.zeros((7, block), F32)], axis=0).astype(BF16)
    right = jnp.concatenate([r_hi, r_hi, r_lo, jnp.zeros((7, channels), F32)], axis=0).astype(BF16)
    out[...] = dot(left, right, ((0,), (0,)))


def finish(own, r1, r2, r3, out):
    z = lax.axis_index("seq") >> 1
    m = own.shape[0] // 2
    for k, ref in enumerate((own, r1, r2, r3)):
        for layer in range(2):
            out[layer, pl.ds(pl.multiple_of((z ^ k) * m, m), m), :] = ref[layer * m : (layer + 1) * m, :].astype(F32)


def scatter_sum(x, n):
    blocks = x.astype(BF16).reshape(n, x.shape[0] // n, x.shape[1])
    got = lax.all_to_all(blocks, "seq", 0, 0, tiled=True)
    return jnp.sum(got.astype(F32), axis=0)


def gather(x, n):
    return lax.all_to_all(jnp.broadcast_to(x[None], (n,) + x.shape), "seq", 0, 0, tiled=True)


def along(x, k):
    n = lax.axis_size("seq")
    return lax.ppermute(x, "seq", [(i, i ^ k) for i in range(n)])


def shape(dims, dtype):
    return jax.ShapeDtypeStruct(dims, dtype)


def all_to_all(x):
    return lax.all_to_all(x, "seq", 0, 0, tiled=True)


def pair_shapes(lead, m, channels):
    dims = (lead, m, channels) if lead else (m, channels)
    return [shape(dims, F32), shape(dims, BF16)]


def limit(mib):
    return pltpu.CompilerParams(vmem_limit_bytes=mib * 2**20)


def after(x, y):
    return lax.optimization_barrier((x, y))[0]


def cost(us):
    return pl.CostEstimate(flops=int(us * 8e8), bytes_accessed=int(us * 3e6), transcendentals=0)


def call(kernel, out_shape, scratch=(), us=1.0):
    def run(*args):
        count = len(out_shape) if isinstance(out_shape, list) else 0
        return pl.pallas_call(
            kernel,
            out_shape=out_shape,
            in_specs=[VMEM] * len(args),
            out_specs=[VMEM] * count if count else VMEM,
            scratch_shapes=list(scratch),
            compiler_params=limit(8),
            cost_estimate=cost(us),
            name=getattr(kernel, "func", kernel).__name__,
        )(*args)

    return run


def body(strain, offsets, dilation, input_weight, conv_weight, conv_bias, out_weight, cotangent):
    rows = strain.shape[1]
    channels = input_weight.shape[1]
    width = conv_weight.shape[3]
    n = lax.axis_size("seq")
    me = lax.axis_index("seq")
    ext = LAG + rows
    scale = 1.0 / math.sqrt(rows * n)
    prev = lax.ppermute(strain, "seq", [(i, i + 1) for i in range(n - 1)])
    weight = jnp.transpose(conv_weight, (0, 2, 1, 3))
    full = ext + LAG + MAXSHIFT
    ow_far = swap(out_weight[0])
    gate0, fa, fb, st, srow, i3 = pl.pallas_call(
        first_layer,
        out_shape=[
            shape((ext, width), BF16),
            shape((ext, width), F32),
            shape((ext, width), F32),
            shape((ext, 32), BF16),
            shape((16, ext), BF16),
            shape((32, channels), BF16),
        ],
        in_specs=[SMEM, SMEM] + [VMEM] * 5,
        out_specs=[VMEM] * 6,
        scratch_shapes=[pltpu.VMEM((8, full), F32), pltpu.VMEM((8, ext), F32)],
        compiler_params=limit(10),
        cost_estimate=cost(2),
        name="first_layer",
    )(offsets, dilation, prev, strain, input_weight, weight, conv_bias)
    gate_far = swap(gate0)
    hm, gg = call(
        functools.partial(own_mix, scale), [shape((ext, channels), F32), shape((rows, width), F32)], us=1.5
    )(st, i3, gate0, out_weight, cotangent)
    part, gl1, gate1, joined, bias1 = pl.pallas_call(
        second_layer,
        out_shape=[
            shape((ext, channels), BF16),
            shape((rows, 2 * width), BF16),
            shape((rows, width), BF16),
            shape((rows, 2 * channels), BF16),
            shape((1, 2 * width), F32),
        ],
        in_specs=[SMEM] + [VMEM] * 6,
        out_specs=[VMEM] * 5,
        scratch_shapes=[
            pltpu.VMEM((ext, channels), F32),
            pltpu.VMEM((ext, channels), F32),
            pltpu.VMEM((rows + 16, channels), F32),
            pltpu.VMEM((rows, 2 * width), F32),
        ],
        compiler_params=limit(28),
        cost_estimate=cost(7),
        name="second_layer",
    )(dilation, hm, gg, gate_far, ow_far, weight, conv_bias)
    apart = swap(part)

    if n == 8:
        o_keep, o_send = call(
            functools.partial(out_grad, scale),
            [shape((4, width // 8, channels), F32), shape((4, width // 8, channels), BF16)],
            [pltpu.VMEM((8, width // 8, channels), F32)],
            0.5,
        )(gate1, cotangent)
        o_got = along(o_send, 1)
        c_keep, c_send = call(
            conv_grad,
            [shape((4, channels // 4, 2 * width), F32), shape((4, channels // 4, 2 * width), BF16)],
            [pltpu.VMEM((8, channels // 4, 2 * width), F32)],
            1.5,
        )(joined, gl1)
        apart = after(apart, c_send)
    out0, small = pl.pallas_call(
        functools.partial(first_back, scale),
        out_shape=[shape((width, channels), BF16), shape((16, 2 * width), F32)],
        in_specs=[VMEM] * 10,
        out_specs=[VMEM] * 2,
        scratch_shapes=[
            pltpu.VMEM((ext, channels), BF16),
            pltpu.VMEM((ext, 2 * width), BF16),
            pltpu.VMEM((ext, width), F32),
        ],
        compiler_params=limit(16),
        cost_estimate=cost(3),
        name="first_back",
    )(part, apart, cotangent, gate0, fa, fb, srow, out_weight, weight, bias1)
    if n == 8:
        m = width // 4
        c_got = along(after(c_send, small), 1)
        back = call(pack, [shape((m + m // 2 + 16, channels), BF16)] * 4, us=0.5)(out0, small, o_keep, o_got)
        got = [along(back[k], 2 * k) for k in (1, 2, 3)]
        c_keep = after(c_keep, back[0])
        c_two, c_send = call(pair_add, pair_shapes(2, channels // 4, 2 * width))(c_keep, c_got)
        c_got = along(c_send, 2)
        quarter = call(quarter_sum, shape(back[0].shape, BF16), [pltpu.VMEM((4,) + back[0].shape, F32)])(back[0], *got)
        other = along(quarter, 1)
        c_own, c_send = call(pair_add_again, pair_shapes(0, channels // 4, 2 * width))(c_two, c_got)
        c_got = along(c_send, 4)
        blocks, small = call(half_sum, [shape((2 * m, channels), BF16), shape((16, channels), F32)])(quarter, other)
        got = [along(blocks, 2 * k) for k in (1, 2, 3)]
        dw1 = c_own + c_got.astype(F32)
        grad_out = call(finish, shape((2, width, channels), F32))(blocks, *got)
    else:
        dw1 = scatter_sum(dot(joined, gl1, ((0,), (0,))), n)
        do1 = scatter_sum(dot(gate1, cotangent, ((0,), (0,))) * scale, n)
        do0 = scatter_sum(out0, n)
        small = jnp.sum(gather(small, n), axis=0)
        do = gather(jnp.stack([do0, do1]).astype(BF16), n).astype(F32)
        grad_out = jnp.moveaxis(do, 0, 1).reshape(2, width, channels)
    r, g, bias = small[: 2 * DET], small[2 * DET : 3 * DET], small[3 * DET : 3 * DET + 2]
    grad_input = g + swap(g)
    grad_bias = bias.reshape(2, 2, width)
    block = 2 * channels // n
    if n == 8:
        dw0 = call(first_conv, shape((block, 2 * width), F32))(input_weight, small)
    else:
        mine_iw = lax.dynamic_slice_in_dim(input_weight, (me * block) % channels, block, 1)
        mine_r = jnp.where(me * block < channels, r[:DET], r[DET:])
        dw0 = sum(mine_iw[k][:, None] * mine_r[k][None, :] for k in range(DET))
    grad_conv = jnp.stack([dw0, dw1]).reshape(2, block, 2, width)
    return (grad_input, grad_conv, grad_bias, grad_out)


def solution(mesh):
    in_specs = (
        P(None, ("groups", "seq")),
        P("groups"),
        P(),
        P(),
        P(None, None, None, "tensor"),
        P(None, None, "tensor"),
        P(None, "tensor", None),
        P(("groups", "seq"), None),
    )
    out_specs = (
        P("groups", None),
        P("groups", "seq", None, "tensor"),
        P("groups", None, "tensor"),
        P("groups", "tensor", None),
    )
    return jax.shard_map(body, mesh=mesh, in_specs=in_specs, out_specs=out_specs, check_vma=False)
```
